128 devices in a mesh: ctx: 16 (over z, y_hi, core), tp: 8 (over y_lo, x).
Axes of the slice: x: 4, y: 4 (y_hi: 2, y_lo: 2; y = y_hi * 2 + y_lo), z: 4, core: 2. Of those that a mesh axis runs over, the one named last changes fastest.
Arguments:
- trunk_out: bfloat16 [8192, 1536], P('ctx', 'tp'), may hold values from -6 to 6
- proj_weight: bfloat16 [1536, 384], replicated, may hold values from -0.15625 to 0.15625
- base_skip: bfloat16 [1048576, 384], P(('ctx', 'tp')), may hold values from -6 to 6
- conv_weight: bfloat16 [2, 3, 384, 384], replicated, may hold values from -0.1875 to 0.1875
- head_hidden: bfloat16 [56, 384, 768], P('tp'), may hold values from -0.3125 to 0.3125
- head_logit: bfloat16 [56, 768], P('tp'), may hold values from -0.21875 to 0.21875
- site_index: int32 [16384], P(('ctx', 'tp')), may hold values from 0 to 8191
- tissue_slot: int32 [54], replicated, may hold values from 0 to 55, as said below
Outputs:
- usage: float32 [54, 16384], P(None, ('ctx', 'tp'))
- tower: bfloat16 [1048576, 384], P(('ctx', 'tp'))
The draws below stay inside these ranges and needn't reach their ends.
Inputs may be any that keep to these rules, and one draw needn't show every extreme that they name: tissue_slot holds 54 different slots of the 56 slots.
All inputs are finite; a program needn't handle non-finite values.
Results may differ from the reference program's by a relative error of at most 0.02.
Values may be sent and summed in bfloat16 or wider, within the bound.
A program may use at most 320 MiB of HBM per device.

```python
import jax
import jax.numpy as jnp
from jax import lax

WIDTH = 1536
CHANNELS = 384
HIDDEN_SIZE = 768
TISSUES = 54
BASES = 128
CAND_DEV = 128
POS_DEV = 8192
DILATION_INITIAL = 1024
DILATION_LATTER = 4096
OWNERS = 8
SLOTS = 7
TOKENS = 8192
POSITIONS = 1048576
CANDIDATES = 16384


def draw_tissue_slot(key, part):
    total_slots = OWNERS * SLOTS
    first_key = jax.random.fold_in(key, 11)
    second_key = jax.random.fold_in(key, 23)
    others = jax.random.permutation(first_key, total_slots - 1)[:TISSUES - 1].astype(jnp.int32)
    values = jnp.concatenate([others, jnp.full((1,), total_slots - 1, jnp.int32)])
    order = jax.random.permutation(second_key, TISSUES)
    return values[order].astype(jnp.int32)


def set_ends(entries, own_key, low, high):
    extent = entries.shape
    place = [jax.random.randint(jax.random.fold_in(own_key, axis), (), 0, extent[axis]) for axis in range(len(extent))]
    entries = entries.at[tuple(place)].set(low)
    longest = extent.index(max(extent))
    place[longest] = (place[longest] + 1) % extent[longest]
    return entries.at[tuple(place)].set(high)


def level_of(rng, extent, cuts, smallest, top_value):
    level, own = 1.0, jax.random.fold_in(rng, 6)
    for axis_at, shards_of in cuts:
        heights = jnp.exp(jax.random.uniform(jax.random.fold_in(own, axis_at), (shards_of,), jnp.float32, smallest / len(cuts), top_value / len(cuts)))
        level = level * jnp.repeat(heights, extent[axis_at] // shards_of).reshape([-1 if axis == axis_at else 1 for axis in range(len(extent))])
    return level


def noise(own_key, shape, width, limit, split=(), kind=jnp.bfloat16):
    factor_of = level_of(own_key, shape, split, -0.22, 0.18) if split else 1.0
    drawn = jax.random.normal(own_key, shape, jnp.float32) * width * factor_of
    return jnp.minimum(jnp.maximum(drawn, -limit), limit).astype(kind)


def setup_inputs(seed: int = 0) -> dict:
    seeds = jax.random.split(jax.random.key(seed), 9)
    return {
        "trunk_out": noise(seeds[0], (TOKENS, WIDTH), 1.0, 6.0, ((0, 16), (1, 8))),
        "proj_weight": noise(seeds[1], (WIDTH, CHANNELS), WIDTH ** -0.5, 0.15625),
        "base_skip": noise(seeds[2], (POSITIONS, CHANNELS), 1.0, 6.0, ((0, 128),)),
        "conv_weight": noise(seeds[3], (2, 3, CHANNELS, CHANNELS), (3 * CHANNELS) ** -0.5, 0.1875),
        "head_hidden": noise(seeds[4], (OWNERS * SLOTS, CHANNELS, HIDDEN_SIZE), CHANNELS ** -0.5, 0.3125, ((0, 8),)),
        "head_logit": noise(seeds[5], (OWNERS * SLOTS, HIDDEN_SIZE), HIDDEN_SIZE ** -0.5, 0.21875, ((0, 8),)),
        "site_index": set_ends(jax.random.randint(seeds[6], (CANDIDATES,), 0, POS_DEV), jax.random.fold_in(seeds[6], 1), 0, POS_DEV - 1).astype(jnp.int32),
        "tissue_slot": draw_tissue_slot(jax.random.fold_in(seeds[8], 71), 0),
    }


EPSILON = 1e-06

def normalize(values):
    wide = values.astype(jnp.float32)
    return wide * lax.rsqrt(lax.optimization_barrier(jnp.mean(wide * wide, axis=-1, keepdims=True)) + EPSILON)

def dilated(padded, weight, tap_spacing, count):
    total = jnp.zeros((count, weight.shape[2]), jnp.float32)
    for offset in range(3):
        window = lax.slice_in_dim(padded, offset * tap_spacing, offset * tap_spacing + count, axis=0)
        total = total + jnp.dot(window, weight[offset], preferred_element_type=jnp.float32)
    return total

def reference(trunk_out, proj_weight, base_skip, conv_weight, head_hidden, head_logit, site_index, tissue_slot):
    projected = jnp.dot(trunk_out, proj_weight, preferred_element_type=jnp.float32)
    upsampled = projected[:, None, :] + base_skip.astype(jnp.float32).reshape(TOKENS, BASES, CHANNELS)
    current = upsampled.reshape(POSITIONS, CHANNELS).astype(jnp.bfloat16)
    for layer_module, tap_spacing in ((0, DILATION_INITIAL), (1, DILATION_LATTER)):
        normed = normalize(current).astype(jnp.bfloat16)
        padded = jnp.pad(normed, ((tap_spacing, tap_spacing), (0, 0)))
        mixed = dilated(padded, conv_weight[layer_module], tap_spacing, POSITIONS)
        current = (current.astype(jnp.float32) + jax.nn.gelu(mixed)).astype(jnp.bfloat16)
    tiles = jnp.arange(CANDIDATES, dtype=jnp.int32) // CAND_DEV
    located = (site_index + tiles * POS_DEV).astype(jnp.int32)
    chosen = normalize(jnp.take(current, located, axis=0)).astype(jnp.bfloat16)

    def one_tissue(slot):
        hidden = jax.nn.gelu(jnp.dot(chosen, head_hidden[slot], preferred_element_type=jnp.float32)).astype(jnp.bfloat16)
        return jnp.dot(hidden, head_logit[slot], preferred_element_type=jnp.float32)
    usage = lax.map(one_tissue, tissue_slot)
    return (usage, current)
```

```python
import functools

import jax
import jax.numpy as jnp
from jax import lax
from jax.experimental import pallas as pl
from jax.experimental.pallas import tpu as pltpu
from jax.sharding import PartitionSpec as P

BASES = 128
EPSILON = 1e-06
MESH = pl.DeviceIdType.MESH
BF16 = jnp.bfloat16
F32 = jnp.float32


def normalize(values):
    wide = values.astype(F32)
    mean = jnp.sum(wide * wide, axis=-1, keepdims=True) * (1.0 / values.shape[-1])
    return (wide * lax.rsqrt(mean + EPSILON)).astype(BF16)


def gelu(x):
    inner = x * (0.7978845608028654 + 0.035677408136300125 * (x * x))
    half = 0.5 * x
    return half + half * jnp.tanh(inner)


def kernel(
    dims,
    trunk, projw, base, convw, headw, headl, site, tissue,
    usage, tower,
    cur, n1, n2, raw, trunk_all, proj, pw, cw, hw, wl, sites, picked, chosen, logit_out, logit_in,
    local_sem, trunk_send, trunk_recv, raw_send, raw_recv, proj_send, proj_recv,
    halo_send, halo_recv, tower_sem, chosen_send, chosen_recv, logit_send, logit_recv,
):
    n_ctx, n_tp, tile, channels, near, far, chunk = dims
    count = far // chunk
    tokens = tile // BASES
    near_tokens = near // BASES
    cands = site.shape[1]
    slots = headl.shape[0]
    ctx = lax.axis_index("ctx")
    tp = lax.axis_index("tp")
    place = ctx * n_tp + tp
    total = n_ctx * n_tp
    left_at = lax.rem(place + total - 1, total)
    right_at = lax.rem(place + 1, total)
    left = {"ctx": left_at // n_tp, "tp": lax.rem(left_at, n_tp)}
    right = {"ctx": right_at // n_tp, "tp": lax.rem(right_at, n_tp)}
    first_tile = place == 0
    last_tile = place == total - 1

    def peer(step):
        return lax.rem(tp + step, n_tp)

    def remote(src, dst, send, recv, device):
        return pltpu.make_async_remote_copy(
            src_ref=src, dst_ref=dst, send_sem=send, recv_sem=recv,
            device_id=device, device_id_type=MESH,
        )

    loads = [
        pltpu.make_async_copy(projw, pw, local_sem.at[0]),
        pltpu.make_async_copy(base, cur, local_sem.at[1]),
        pltpu.make_async_copy(convw, cw, local_sem.at[2]),
        pltpu.make_async_copy(headw, hw, local_sem.at[3]),
        pltpu.make_async_copy(
            trunk.at[pl.ds(tp * tokens, tokens)], trunk_all.at[tp], local_sem.at[4]
        ),
    ]
    loads[4].start()
    for load in loads[:4]:
        load.start()

    barrier = pltpu.get_barrier_semaphore()
    for device in (left, right):
        pl.semaphore_signal(barrier, inc=1, device_id=device, device_id_type=MESH)
    for step in range(1, n_tp):
        pl.semaphore_signal(
            barrier, inc=1, device_id={"ctx": ctx, "tp": peer(step)}, device_id_type=MESH
        )
    pl.semaphore_wait(barrier, n_tp + 1)

    trunk_copies = []
    for step in range(1, n_tp):
        to = peer(step)
        copy = remote(
            trunk.at[pl.ds(to * tokens, tokens)], trunk_all.at[tp],
            trunk_send.at[step - 1], trunk_recv.at[step - 1], {"ctx": ctx, "tp": to},
        )
        copy.start()
        trunk_copies.append(copy)
    raw_copies = [
        remote(base.at[pl.ds(tile - near, near)], raw.at[0], raw_send.at[0], raw_recv.at[0], right),
        remote(base.at[pl.ds(0, near)], raw.at[1], raw_send.at[1], raw_recv.at[1], left),
    ]
    for copy in raw_copies:
        copy.start()

    sites[...] = jnp.broadcast_to(site[...], (cands, cands)).T
    wl[...] = jnp.zeros_like(wl)
    wl[pl.ds(0, slots), :] = headl[...].astype(F32)
    picked[...] = jnp.zeros_like(picked)

    loads[4].wait()
    loads[0].wait()
    total_proj = jnp.dot(trunk_all[tp], pw[tp], preferred_element_type=F32)
    for step in range(1, n_tp):
        trunk_copies[step - 1].wait_recv()
        source = lax.rem(tp + n_tp - step, n_tp)
        total_proj += jnp.dot(trunk_all[source], pw[source], preferred_element_type=F32)
    proj[pl.ds(near_tokens, tokens), :] = total_proj
    loads[1].wait()

    def add_token(token, rows, at_proj):
        lifted = rows.astype(F32) + proj[pl.ds(at_proj, 1), :]
        return lifted.astype(BF16)

    def own_rows(step, carry):
        for part in range(2):
            token = step * 2 + part
            at = pl.multiple_of(token * BASES, BASES)
            value = add_token(token, cur[pl.ds(at, BASES), :], token + near_tokens)
            cur[pl.ds(at, BASES), :] = value
            n1[pl.ds(at + near, BASES), :] = normalize(value)
        return carry

    lax.fori_loop(0, tokens // 4, own_rows, 0)
    proj_copies = [
        remote(
            proj.at[pl.ds(tokens, near_tokens)], proj.at[pl.ds(0, near_tokens)],
            proj_send.at[0], proj_recv.at[0], right,
        ),
        remote(
            proj.at[pl.ds(near_tokens, near_tokens)],
            proj.at[pl.ds(tokens + near_tokens, near_tokens)],
            proj_send.at[1], proj_recv.at[1], left,
        ),
    ]
    for copy in proj_copies:
        copy.start()
    lax.fori_loop(tokens // 4, tokens // 2, own_rows, 0)
    loads[2].wait()

    def pair_of(ref, at):
        return jnp.concatenate(
            [
                ref[pl.ds(pl.multiple_of(at, chunk), chunk), :],
                ref[pl.ds(pl.multiple_of(at + far, chunk), chunk), :],
            ],
            axis=0,
        )

    def chunk_of(step):
        return lax.rem(step + near // chunk, count)

    def halo_copy(index, side):
        at = pl.multiple_of(index * chunk, chunk)
        if side == 0:
            return remote(
                n2.at[pl.ds(at + 2 * far, chunk)], n2.at[pl.ds(at, chunk)],
                halo_send.at[0, index], halo_recv.at[0, index], right,
            )
        return remote(
            n2.at[pl.ds(at + far, chunk)], n2.at[pl.ds(at + 3 * far, chunk)],
            halo_send.at[1, index], halo_recv.at[1, index], left,
        )

    def send_chunk(step):
        index = chunk_of(step)
        halo_copy(index, 0).start()
        halo_copy(index, 1).start()

    def block_one(step, carry):
        at = pl.multiple_of(chunk_of(step) * chunk, chunk)
        window = jnp.concatenate(
            [pair_of(n1, at), pair_of(n1, at + near), pair_of(n1, at + 2 * near)], axis=1
        )
        mixed = jnp.dot(window, cw[0], preferred_element_type=F32)
        value = (pair_of(cur, at).astype(F32) + gelu(mixed)).astype(BF16)
        scaled = normalize(value)
        for part in range(2):
            rows = slice(part * chunk, (part + 1) * chunk)
            cur[pl.ds(at + part * far, chunk), :] = value[rows]
            n2[pl.ds(at + (part + 1) * far, chunk), :] = scaled[rows]

        @pl.when(step > 0)
        def _():
            send_chunk(step - 1)

        return carry

    middle = (far - near) // chunk - near // chunk
    lax.fori_loop(0, middle, block_one, 0)

    for copy in raw_copies:
        copy.wait_recv()
    for copy in proj_copies:
        copy.wait_recv()

    def halo_rows(step, carry):
        at = pl.multiple_of(step * BASES, BASES)
        low = normalize(add_token(step, raw[0, pl.ds(at, BASES), :], step))
        n1[pl.ds(at, BASES), :] = jnp.where(first_tile, jnp.zeros_like(low), low)
        high = normalize(
            add_token(step, raw[1, pl.ds(at, BASES), :], step + tokens + near_tokens)
        )
        n1[pl.ds(at + tile + near, BASES), :] = jnp.where(last_tile, jnp.zeros_like(high), high)
        return carry

    lax.fori_loop(0, near_tokens, halo_rows, 0)
    lax.fori_loop(middle, count, block_one, 0)
    send_chunk(count - 1)

    lane = lax.broadcasted_iota(jnp.int32, (cands, chunk), 1)
    site_wide = jnp.concatenate([sites[...]] * (chunk // cands), axis=1)

    def tower_copy(index, part):
        rows = pl.ds(pl.multiple_of(index * chunk + part * far, chunk), chunk)
        return pltpu.make_async_copy(cur.at[rows], tower.at[rows], tower_sem.at[part, index])

    def block_two(step, carry):
        index = chunk_of(step)
        at = pl.multiple_of(index * chunk, chunk)
        halo_copy(index, 0).wait_recv()
        halo_copy(index, 1).wait_recv()
        low = n2[pl.ds(at, chunk), :]
        low = jnp.where(first_tile, jnp.zeros_like(low), low)
        one = n2[pl.ds(at + far, chunk), :]
        two = n2[pl.ds(at + 2 * far, chunk), :]
        high = n2[pl.ds(at + 3 * far, chunk), :]
        high = jnp.where(last_tile, jnp.zeros_like(high), high)
        window = jnp.concatenate(
            [
                jnp.concatenate([low, one], axis=0),
                jnp.concatenate([one, two], axis=0),
                jnp.concatenate([two, high], axis=0),
            ],
            axis=1,
        )
        mixed = jnp.dot(window, cw[1], preferred_element_type=F32)
        value = (pair_of(cur, at).astype(F32) + gelu(mixed)).astype(BF16)
        for part in range(2):
            cur[pl.ds(at + part * far, chunk), :] = value[part * chunk:(part + 1) * chunk]
        hits = jnp.concatenate(
            [
                jnp.where(site_wide == lane + (at + part * far), 1.0, 0.0).astype(BF16)
                for part in range(2)
            ],
            axis=1,
        )
        picked[...] += jnp.dot(hits, value, preferred_element_type=F32)
        for part in range(2):
            tower_copy(index, part).start()
        return carry

    lax.fori_loop(0, count, block_two, 0)
    loads[3].wait()
    chosen[tp] = normalize(picked[...])

    def drain(index, carry):
        for side in range(2):
            halo_copy(index, side).wait_send()
        return carry

    lax.fori_loop(0, count, drain, 0)

    def chosen_copy(step):
        return remote(
            chosen.at[tp], chosen.at[tp], chosen_send.at[step - 1], chosen_recv.at[step - 1],
            {"ctx": ctx, "tp": peer(step)},
        )

    for step in range(1, n_tp):
        chosen_copy(step).start()

    def logit_copy(to):
        step = lax.rem(to + n_tp - tp, n_tp)
        return remote(
            logit_out.at[pl.ds(pl.multiple_of(to * 8, 8), 8)],
            logit_in.at[pl.ds(pl.multiple_of(tp * 8, 8), 8)],
            logit_send.at[step - 1], logit_recv.at[step - 1], {"ctx": ctx, "tp": to},
        )

    row = lax.broadcasted_iota(jnp.int32, wl.shape, 0)

    def heads(step, carry):
        pair = lax.rem(tp // 2 + step, n_tp // 2)
        for part in range(2):
            source = pair * 2 + part

            @pl.when(source != tp)
            def _():
                away = lax.rem(tp + n_tp - source, n_tp)
                remote(
                    chosen.at[source], chosen.at[source],
                    chosen_send.at[away - 1], chosen_recv.at[away - 1], {"ctx": ctx, "tp": source},
                ).wait_recv()

        rows_in = jnp.concatenate([chosen[pair * 2], chosen[pair * 2 + 1]], axis=0)
        scores = jnp.zeros((8, 2 * cands), F32)
        for slot in range(slots):
            hidden = gelu(jnp.dot(rows_in, hw[slot], preferred_element_type=F32)).astype(BF16)
            weights = jnp.where(row == slot, wl[...], 0.0).astype(BF16)
            scores += lax.dot_general(
                weights, hidden, (((1,), (1,)), ((), ())), preferred_element_type=F32
            )
        for part in range(2):
            source = pair * 2 + part
            logit_out[pl.ds(pl.multiple_of(source * 8, 8), 8), :] = (
                scores[:, part * cands:(part + 1) * cands]
            )
        for part in range(2):
            source = pair * 2 + part

            @pl.when(source != tp)
            def _():
                logit_copy(source).start()

        return carry

    lax.fori_loop(0, n_tp // 2, heads, 0)
    own = pl.ds(pl.multiple_of(tp * 8, 8), 8)
    logit_in[own, :] = logit_out[own, :]
    for step in range(1, n_tp):
        chosen_copy(step).wait_send()
        trunk_copies[step - 1].wait_send()
    for copy in raw_copies + proj_copies:
        copy.wait_send()

    def drain_tower(index, carry):
        for part in range(2):
            tower_copy(index, part).wait()
        return carry

    lax.fori_loop(0, count, drain_tower, 0)
    for step in range(1, n_tp):
        copy = logit_copy(peer(step))
        copy.wait_send()
        copy.wait_recv()
    for tissue_at in range(usage.shape[0]):
        slot = tissue[tissue_at]
        at = (slot // slots) * 8 + lax.rem(slot, slots)
        usage[pl.ds(tissue_at, 1), :] = logit_in[pl.ds(at, 1), :]


def on_device(
    n_ctx, n_tp,
    trunk_out, proj_weight, base_skip, conv_weight, head_hidden, head_logit, site_index, tissue_slot,
):
    tile, channels = base_skip.shape
    width = proj_weight.shape[0]
    near, far, chunk = tile // 8, tile // 2, 256
    count = far // chunk
    tokens = tile // BASES
    near_tokens = near // BASES
    cands = site_index.shape[0]
    slots, _, hidden = head_hidden.shape
    tissues = tissue_slot.shape[0]
    share = width // n_tp
    dims = (n_ctx, n_tp, tile, channels, near, far, chunk)
    anywhere = pl.BlockSpec(memory_space=pl.ANY)
    vmem = pl.BlockSpec(memory_space=pltpu.VMEM)
    smem = pl.BlockSpec(memory_space=pltpu.SMEM)
    dma = pltpu.SemaphoreType.DMA
    usage, tower = pl.pallas_call(
        functools.partial(kernel, dims),
        out_shape=(
            jax.ShapeDtypeStruct((tissues, cands), F32),
            jax.ShapeDtypeStruct((tile, channels), BF16),
        ),
        in_specs=[anywhere] * 5 + [vmem, vmem, smem],
        out_specs=(vmem, anywhere),
        scratch_shapes=[
            pltpu.VMEM((tile, channels), BF16),
            pltpu.VMEM((tile + 2 * near, channels), BF16),
            pltpu.VMEM((tile + 2 * far, channels), BF16),
            pltpu.VMEM((2, near, channels), BF16),
            pltpu.VMEM((n_tp, tokens, share), BF16),
            pltpu.VMEM((tokens + 2 * near_tokens, channels), F32),
            pltpu.VMEM((n_tp, share, channels), BF16),
            pltpu.VMEM((2, 3 * channels, channels), BF16),
            pltpu.VMEM((slots, channels, hidden), BF16),
            pltpu.VMEM((8, hidden), F32),
            pltpu.VMEM((cands, cands), jnp.int32),
            pltpu.VMEM((cands, channels), F32),
            pltpu.VMEM((n_tp, cands, channels), BF16),
            pltpu.VMEM((n_tp * 8, cands), F32),
            pltpu.VMEM((n_tp * 8, cands), F32),
            dma((5,)), dma((n_tp - 1,)), dma((n_tp - 1,)), dma((2,)), dma((2,)), dma((2,)), dma((2,)),
            dma((2, count)), dma((2, count)), dma((2, count)),
            dma((n_tp - 1,)), dma((n_tp - 1,)), dma((n_tp - 1,)), dma((n_tp - 1,)),
        ],
        compiler_params=pltpu.CompilerParams(
            collective_id=0, has_side_effects=True, vmem_limit_bytes=60 * 1024 * 1024
        ),
    )(
        trunk_out,
        proj_weight.reshape(n_tp, share, channels),
        base_skip,
        conv_weight.reshape(2, 3 * channels, channels),
        head_hidden,
        head_logit,
        site_index.reshape(1, cands),
        tissue_slot,
    )
    return usage, tower


def solution(mesh):
    return jax.shard_map(
        functools.partial(on_device, mesh.shape["ctx"], mesh.shape["tp"]),
        mesh=mesh,
        in_specs=(
            P("ctx", "tp"),
            P(),
            P(("ctx", "tp"), None),
            P(),
            P("tp", None, None),
            P("tp", None),
            P(("ctx", "tp")),
            P(),
        ),
        out_specs=(P(None, ("ctx", "tp")), P(("ctx", "tp"), None)),
        check_vma=False,
    )
```

```python
import functools

import jax
import jax.numpy as jnp
from jax import lax
from jax.experimental import pallas as pl
from jax.experimental.pallas import tpu as pltpu
from jax.sharding import PartitionSpec as P

BASES = 128
EPSILON = 1e-06
MESH = pl.DeviceIdType.MESH
BF16 = jnp.bfloat16
F32 = jnp.float32


def normalize(values):
    wide = values.astype(F32)
    mean = jnp.sum(wide * wide, axis=-1, keepdims=True) * (1.0 / values.shape[-1])
    return (wide * lax.rsqrt(mean + EPSILON)).astype(BF16)


def gelu(x):
    inner = x * (0.7978845608028654 + 0.035677408136300125 * (x * x))
    half = 0.5 * x
    return half + half * jnp.tanh(inner)


def kernel(
    dims,
    trunk, projw, base, convw, headw, headl, site, tissue,
    usage, tower,
    cur, n1, n2, raw, trunk_all, proj, pw, cw, hw, wl, sites, picked, chosen, logit_out, logit_in,
    local_sem, trunk_send, trunk_recv, raw_send, raw_recv, proj_send, proj_recv,
    halo_send, halo_recv, tower_sem, chosen_send, chosen_recv, logit_send, logit_recv,
):
    n_ctx, n_tp, tile, channels, near, far, chunk = dims
    count = far // chunk
    tokens = tile // BASES
    near_tokens = near // BASES
    cands = site.shape[1]
    slots = headl.shape[0]
    ctx = lax.axis_index("ctx")
    tp = lax.axis_index("tp")
    place = ctx * n_tp + tp
    total = n_ctx * n_tp
    left_at = lax.rem(place + total - 1, total)
    right_at = lax.rem(place + 1, total)
    left = {"ctx": left_at // n_tp, "tp": lax.rem(left_at, n_tp)}
    right = {"ctx": right_at // n_tp, "tp": lax.rem(right_at, n_tp)}
    first_tile = place == 0
    last_tile = place == total - 1

    def peer(step):
        return lax.rem(tp + step, n_tp)

    def remote(src, dst, send, recv, device):
        return pltpu.make_async_remote_copy(
            src_ref=src, dst_ref=dst, send_sem=send, recv_sem=recv,
            device_id=device, device_id_type=MESH,
        )

    loads = [
        pltpu.make_async_copy(projw, pw, local_sem.at[0]),
        pltpu.make_async_copy(base, cur, local_sem.at[1]),
        pltpu.make_async_copy(convw, cw, local_sem.at[2]),
        pltpu.make_async_copy(headw, hw, local_sem.at[3]),
        pltpu.make_async_copy(
            trunk.at[pl.ds(tp * tokens, tokens)], trunk_all.at[tp], local_sem.at[4]
        ),
    ]
    loads[4].start()
    for load in loads[:4]:
        load.start()

    barrier = pltpu.get_barrier_semaphore()
    for device in (left, right):
        pl.semaphore_signal(barrier, inc=1, device_id=device, device_id_type=MESH)
    for step in range(1, n_tp):
        pl.semaphore_signal(
            barrier, inc=1, device_id={"ctx": ctx, "tp": peer(step)}, device_id_type=MESH
        )
    pl.semaphore_wait(barrier, n_tp + 1)

    trunk_copies = []
    for step in range(1, n_tp):
        to = peer(step)
        copy = remote(
            trunk.at[pl.ds(to * tokens, tokens)], trunk_all.at[tp],
            trunk_send.at[step - 1], trunk_recv.at[step - 1], {"ctx": ctx, "tp": to},
        )
        copy.start()
        trunk_copies.append(copy)
    raw_copies = [
        remote(base.at[pl.ds(tile - near, near)], raw.at[0], raw_send.at[0], raw_recv.at[0], right),
        remote(base.at[pl.ds(0, near)], raw.at[1], raw_send.at[1], raw_recv.at[1], left),
    ]
    def both(low, high):
        pl.when(jnp.logical_not(first_tile))(low)
        pl.when(jnp.logical_not(last_tile))(high)

    both(raw_copies[1].start, raw_copies[0].start)

    sites[...] = jnp.broadcast_to(site[...], (cands, cands)).T
    wl[...] = jnp.zeros_like(wl)
    wl[pl.ds(0, slots), :] = headl[...].astype(F32)
    picked[...] = jnp.zeros_like(picked)

    loads[4].wait()
    loads[0].wait()
    total_proj = jnp.dot(trunk_all[tp], pw[tp], preferred_element_type=F32)
    for step in range(1, n_tp):
        trunk_copies[step - 1].wait_recv()
        source = lax.rem(tp + n_tp - step, n_tp)
        total_proj += jnp.dot(trunk_all[source], pw[source], preferred_element_type=F32)
    proj[pl.ds(near_tokens, tokens), :] = total_proj
    loads[1].wait()

    def add_token(token, rows, at_proj):
        lifted = rows.astype(F32) + proj[pl.ds(at_proj, 1), :]
        return lifted.astype(BF16)

    def own_rows(step, carry):
        for part in range(2):
            token = step * 2 + part
            at = pl.multiple_of(token * BASES, BASES)
            value = add_token(token, cur[pl.ds(at, BASES), :], token + near_tokens)
            cur[pl.ds(at, BASES), :] = value
            n1[pl.ds(at + near, BASES), :] = normalize(value)
        return carry

    lax.fori_loop(0, tokens // 4, own_rows, 0)
    proj_copies = [
        remote(
            proj.at[pl.ds(tokens, near_tokens)], proj.at[pl.ds(0, near_tokens)],
            proj_send.at[0], proj_recv.at[0], right,
        ),
        remote(
            proj.at[pl.ds(near_tokens, near_tokens)],
            proj.at[pl.ds(tokens + near_tokens, near_tokens)],
            proj_send.at[1], proj_recv.at[1], left,
        ),
    ]
    both(proj_copies[1].start, proj_copies[0].start)
    lax.fori_loop(tokens // 4, tokens // 2, own_rows, 0)
    loads[2].wait()

    def pair_of(ref, at):
        return jnp.concatenate(
            [
                ref[pl.ds(pl.multiple_of(at, chunk), chunk), :],
                ref[pl.ds(pl.multiple_of(at + far, chunk), chunk), :],
            ],
            axis=0,
        )

    def chunk_of(step):
        return lax.rem(step + near // chunk, count)

    def halo_copy(index, side):
        at = pl.multiple_of(index * chunk, chunk)
        if side == 0:
            return remote(
                n2.at[pl.ds(at + 2 * far, chunk)], n2.at[pl.ds(at, chunk)],
                halo_send.at[0, index], halo_recv.at[0, index], right,
            )
        return remote(
            n2.at[pl.ds(at + far, chunk)], n2.at[pl.ds(at + 3 * far, chunk)],
            halo_send.at[1, index], halo_recv.at[1, index], left,
        )

    def send_chunk(step):
        index = chunk_of(step)
        both(halo_copy(index, 1).start, halo_copy(index, 0).start)

    def block_one(step, carry):
        at = pl.multiple_of(chunk_of(step) * chunk, chunk)
        window = jnp.concatenate(
            [pair_of(n1, at), pair_of(n1, at + near), pair_of(n1, at + 2 * near)], axis=1
        )
        mixed = jnp.dot(window, cw[0], preferred_element_type=F32)
        value = (pair_of(cur, at).astype(F32) + gelu(mixed)).astype(BF16)
        scaled = normalize(value)
        for part in range(2):
            rows = slice(part * chunk, (part + 1) * chunk)
            cur[pl.ds(at + part * far, chunk), :] = value[rows]
            n2[pl.ds(at + (part + 1) * far, chunk), :] = scaled[rows]

        @pl.when(step > 0)
        def _():
            send_chunk(step - 1)

        return carry

    middle = (far - near) // chunk - near // chunk
    lax.fori_loop(0, middle, block_one, 0)

    for side, edge in ((0, first_tile), (1, last_tile)):
        start = side * (tile + near)

        @pl.when(edge)
        def _():
            n1[pl.ds(start, near), :] = jnp.zeros((near, channels), BF16)
            n2[pl.ds(side * 3 * far, far), :] = jnp.zeros((far, channels), BF16)

        @pl.when(jnp.logical_not(edge))
        def _():
            raw_copies[side].wait_recv()
            proj_copies[side].wait_recv()

            def halo_rows(step, carry):
                at = pl.multiple_of(step * BASES, BASES)
                token = step + side * (tokens + near_tokens)
                n1[pl.ds(at + start, BASES), :] = normalize(
                    add_token(token, raw[side, pl.ds(at, BASES), :], token)
                )
                return carry

            lax.fori_loop(0, near_tokens, halo_rows, 0)

    lax.fori_loop(middle, count, block_one, 0)
    send_chunk(count - 1)

    lane = lax.broadcasted_iota(jnp.int32, (cands, chunk), 1)
    site_wide = jnp.concatenate([sites[...]] * (chunk // cands), axis=1)

    def tower_copy(index, part):
        rows = pl.ds(pl.multiple_of(index * chunk + part * far, chunk), chunk)
        return pltpu.make_async_copy(cur.at[rows], tower.at[rows], tower_sem.at[part, index])

    def block_two(step, carry):
        index = chunk_of(step)
        at = pl.multiple_of(index * chunk, chunk)
        both(halo_copy(index, 0).wait_recv, halo_copy(index, 1).wait_recv)
        low = n2[pl.ds(at, chunk), :]
        one = n2[pl.ds(at + far, chunk), :]
        two = n2[pl.ds(at + 2 * far, chunk), :]
        high = n2[pl.ds(at + 3 * far, chunk), :]
        window = jnp.concatenate(
            [
                jnp.concatenate([low, one], axis=0),
                jnp.concatenate([one, two], axis=0),
                jnp.concatenate([two, high], axis=0),
            ],
            axis=1,
        )
        mixed = jnp.dot(window, cw[1], preferred_element_type=F32)
        value = (pair_of(cur, at).astype(F32) + gelu(mixed)).astype(BF16)
        for part in range(2):
            cur[pl.ds(at + part * far, chunk), :] = value[part * chunk:(part + 1) * chunk]
        hits = jnp.concatenate(
            [
                jnp.where(site_wide == lane + (at + part * far), 1.0, 0.0).astype(BF16)
                for part in range(2)
            ],
            axis=1,
        )
        picked[...] += jnp.dot(hits, value, preferred_element_type=F32)
        for part in range(2):
            tower_copy(index, part).start()
        return carry

    lax.fori_loop(0, count, block_two, 0)
    loads[3].wait()
    chosen[tp] = normalize(picked[...])

    def drain(index, carry):
        both(halo_copy(index, 1).wait_send, halo_copy(index, 0).wait_send)
        return carry

    lax.fori_loop(0, count, drain, 0)

    def chosen_copy(step):
        return remote(
            chosen.at[tp], chosen.at[tp], chosen_send.at[step - 1], chosen_recv.at[step - 1],
            {"ctx": ctx, "tp": peer(step)},
        )

    for step in range(1, n_tp):
        chosen_copy(step).start()

    def logit_copy(to):
        step = lax.rem(to + n_tp - tp, n_tp)
        return remote(
            logit_out.at[pl.ds(pl.multiple_of(to * 8, 8), 8)],
            logit_in.at[pl.ds(pl.multiple_of(tp * 8, 8), 8)],
            logit_send.at[step - 1], logit_recv.at[step - 1], {"ctx": ctx, "tp": to},
        )

    row = lax.broadcasted_iota(jnp.int32, wl.shape, 0)

    def heads(step, carry):
        pair = lax.rem(tp // 2 + step, n_tp // 2)
        for part in range(2):
            source = pair * 2 + part

            @pl.when(source != tp)
            def _():
                away = lax.rem(tp + n_tp - source, n_tp)
                remote(
                    chosen.at[source], chosen.at[source],
                    chosen_send.at[away - 1], chosen_recv.at[away - 1], {"ctx": ctx, "tp": source},
                ).wait_recv()

        rows_in = jnp.concatenate([chosen[pair * 2], chosen[pair * 2 + 1]], axis=0)
        scores = jnp.zeros((8, 2 * cands), F32)
        for slot in range(slots):
            hidden = gelu(jnp.dot(rows_in, hw[slot], preferred_element_type=F32)).astype(BF16)
            weights = jnp.where(row == slot, wl[...], 0.0).astype(BF16)
            scores += lax.dot_general(
                weights, hidden, (((1,), (1,)), ((), ())), preferred_element_type=F32
            )
        for part in range(2):
            source = pair * 2 + part
            logit_out[pl.ds(pl.multiple_of(source * 8, 8), 8), :] = (
                scores[:, part * cands:(part + 1) * cands]
            )
        for part in range(2):
            source = pair * 2 + part

            @pl.when(source != tp)
            def _():
                logit_copy(source).start()

        return carry

    lax.fori_loop(0, n_tp // 2, heads, 0)
    own = pl.ds(pl.multiple_of(tp * 8, 8), 8)
    logit_in[own, :] = logit_out[own, :]
    for step in range(1, n_tp):
        chosen_copy(step).wait_send()
        trunk_copies[step - 1].wait_send()
    for copies in (raw_copies, proj_copies):
        both(copies[1].wait_send, copies[0].wait_send)

    def drain_tower(index, carry):
        for part in range(2):
            tower_copy(index, part).wait()
        return carry

    lax.fori_loop(0, count, drain_tower, 0)
    for step in range(1, n_tp):
        copy = logit_copy(peer(step))
        copy.wait_send()
        copy.wait_recv()
    for tissue_at in range(usage.shape[0]):
        slot = tissue[tissue_at]
        at = (slot // slots) * 8 + lax.rem(slot, slots)
        usage[pl.ds(tissue_at, 1), :] = logit_in[pl.ds(at, 1), :]


def on_device(
    n_ctx, n_tp,
    trunk_out, proj_weight, base_skip, conv_weight, head_hidden, head_logit, site_index, tissue_slot,
):
    tile, channels = base_skip.shape
    width = proj_weight.shape[0]
    near, far, chunk = tile // 8, tile // 2, 256
    count = far // chunk
    tokens = tile // BASES
    near_tokens = near // BASES
    cands = site_index.shape[0]
    slots, _, hidden = head_hidden.shape
    tissues = tissue_slot.shape[0]
    share = width // n_tp
    dims = (n_ctx, n_tp, tile, channels, near, far, chunk)
    anywhere = pl.BlockSpec(memory_space=pl.ANY)
    vmem = pl.BlockSpec(memory_space=pltpu.VMEM)
    smem = pl.BlockSpec(memory_space=pltpu.SMEM)
    dma = pltpu.SemaphoreType.DMA
    usage, tower = pl.pallas_call(
        functools.partial(kernel, dims),
        out_shape=(
            jax.ShapeDtypeStruct((tissues, cands), F32),
            jax.ShapeDtypeStruct((tile, channels), BF16),
        ),
        in_specs=[anywhere] * 5 + [vmem, vmem, smem],
        out_specs=(vmem, anywhere),
        scratch_shapes=[
            pltpu.VMEM((tile, channels), BF16),
            pltpu.VMEM((tile + 2 * near, channels), BF16),
            pltpu.VMEM((tile + 2 * far, channels), BF16),
            pltpu.VMEM((2, near, channels), BF16),
            pltpu.VMEM((n_tp, tokens, share), BF16),
            pltpu.VMEM((tokens + 2 * near_tokens, channels), F32),
            pltpu.VMEM((n_tp, share, channels), BF16),
            pltpu.VMEM((2, 3 * channels, channels), BF16),
            pltpu.VMEM((slots, channels, hidden), BF16),
            pltpu.VMEM((8, hidden), F32),
            pltpu.VMEM((cands, cands), jnp.int32),
            pltpu.VMEM((cands, channels), F32),
            pltpu.VMEM((n_tp, cands, channels), BF16),
            pltpu.VMEM((n_tp * 8, cands), F32),
            pltpu.VMEM((n_tp * 8, cands), F32),
            dma((5,)), dma((n_tp - 1,)), dma((n_tp - 1,)), dma((2,)), dma((2,)), dma((2,)), dma((2,)),
            dma((2, count)), dma((2, count)), dma((2, count)),
            dma((n_tp - 1,)), dma((n_tp - 1,)), dma((n_tp - 1,)), dma((n_tp - 1,)),
        ],
        compiler_params=pltpu.CompilerParams(
            collective_id=0, has_side_effects=True, vmem_limit_bytes=60 * 1024 * 1024
        ),
    )(
        trunk_out,
        proj_weight.reshape(n_tp, share, channels),
        base_skip,
        conv_weight.reshape(2, 3 * channels, channels),
        head_hidden,
        head_logit,
        site_index.reshape(1, cands),
        tissue_slot,
    )
    return usage, tower


def solution(mesh):
    return jax.shard_map(
        functools.partial(on_device, mesh.shape["ctx"], mesh.shape["tp"]),
        mesh=mesh,
        in_specs=(
            P("ctx", "tp"),
            P(),
            P(("ctx", "tp"), None),
            P(),
            P("tp", None, None),
            P("tp", None),
            P(("ctx", "tp")),
            P(),
        ),
        out_specs=(P(None, ("ctx", "tp")), P(("ctx", "tp"), None)),
        check_vma=False,
    )
```

```python
import functools

import jax
import jax.numpy as jnp
from jax import lax
from jax.experimental import pallas as pl
from jax.experimental.pallas import tpu as pltpu
from jax.sharding import PartitionSpec as P

BASES = 128
EPSILON = 1e-06
MESH = pl.DeviceIdType.MESH
BF16 = jnp.bfloat16
F32 = jnp.float32


def normalize(values):
    wide = values.astype(F32)
    mean = jnp.sum(wide * wide, axis=-1, keepdims=True) * (1.0 / values.shape[-1])
    return (wide * lax.rsqrt(mean + EPSILON)).astype(BF16)


def gelu(x):
    inner = x * (0.7978845608028654 + 0.035677408136300125 * (x * x))
    half = 0.5 * x
    return half + half * jnp.tanh(inner)


def kernel(
    dims,
    trunk, projw, base, convw, headw, headl, site, tissue,
    usage, tower,
    cur, n1, n2, raw, trunk_all, proj, pw, cw, hw, wl, sites, picked, chosen, logit_out, logit_in,
    local_sem, trunk_send, trunk_recv, raw_send, raw_recv, proj_send, proj_recv,
    halo_send, halo_recv, tower_sem, chosen_send, chosen_recv, logit_send, logit_recv,
):
    n_ctx, n_tp, tile, channels, near, far, chunk = dims
    count = far // chunk
    tokens = tile // BASES
    near_tokens = near // BASES
    cands = site.shape[1]
    slots = headl.shape[0]
    ctx = lax.axis_index("ctx")
    tp = lax.axis_index("tp")
    place = ctx * n_tp + tp
    total = n_ctx * n_tp
    left_at = lax.rem(place + total - 1, total)
    right_at = lax.rem(place + 1, total)
    left = {"ctx": left_at // n_tp, "tp": lax.rem(left_at, n_tp)}
    right = {"ctx": right_at // n_tp, "tp": lax.rem(right_at, n_tp)}
    first_tile = place == 0
    last_tile = place == total - 1

    def peer(step):
        return lax.rem(tp + step, n_tp)

    def remote(src, dst, send, recv, device):
        return pltpu.make_async_remote_copy(
            src_ref=src, dst_ref=dst, send_sem=send, recv_sem=recv,
            device_id=device, device_id_type=MESH,
        )

    loads = [
        pltpu.make_async_copy(projw, pw, local_sem.at[0]),
        pltpu.make_async_copy(base, cur, local_sem.at[1]),
        pltpu.make_async_copy(convw, cw, local_sem.at[2]),
        pltpu.make_async_copy(headw, hw, local_sem.at[3]),
        pltpu.make_async_copy(
            trunk.at[pl.ds(tp * tokens, tokens)], trunk_all.at[tp], local_sem.at[4]
        ),
    ]
    loads[4].start()
    for load in loads[:4]:
        load.start()

    barrier = pltpu.get_barrier_semaphore()
    for device in (left, right):
        pl.semaphore_signal(barrier, inc=1, device_id=device, device_id_type=MESH)
    for step in range(1, n_tp):
        pl.semaphore_signal(
            barrier, inc=1, device_id={"ctx": ctx, "tp": peer(step)}, device_id_type=MESH
        )
    pl.semaphore_wait(barrier, n_tp + 1)

    trunk_copies = []
    for step in range(1, n_tp):
        to = peer(step)
        copy = remote(
            trunk.at[pl.ds(to * tokens, tokens)], trunk_all.at[tp],
            trunk_send.at[step - 1], trunk_recv.at[step - 1], {"ctx": ctx, "tp": to},
        )
        copy.start()
        trunk_copies.append(copy)
    raw_copies = [
        remote(base.at[pl.ds(tile - near, near)], raw.at[0], raw_send.at[0], raw_recv.at[0], right),
        remote(base.at[pl.ds(0, near)], raw.at[1], raw_send.at[1], raw_recv.at[1], left),
    ]
    def both(low, high):
        pl.when(jnp.logical_not(first_tile))(low)
        pl.when(jnp.logical_not(last_tile))(high)

    both(raw_copies[1].start, raw_copies[0].start)

    sites[...] = jnp.broadcast_to(site[...], (cands, cands)).T
    wl[...] = jnp.zeros_like(wl)
    wl[pl.ds(0, slots), :] = headl[...].astype(F32)
    picked[...] = jnp.zeros_like(picked)

    loads[4].wait()
    loads[0].wait()
    total_proj = jnp.dot(trunk_all[tp], pw[tp], preferred_element_type=F32)
    for step in range(1, n_tp):
        trunk_copies[step - 1].wait_recv()
        source = lax.rem(tp + n_tp - step, n_tp)
        total_proj += jnp.dot(trunk_all[source], pw[source], preferred_element_type=F32)
    proj[pl.ds(near_tokens, tokens), :] = total_proj
    loads[1].wait()

    def add_token(token, rows, at_proj):
        lifted = rows.astype(F32) + proj[pl.ds(at_proj, 1), :]
        return lifted.astype(BF16)

    def own_rows(step, carry):
        for part in range(2):
            token = step * 2 + part
            at = pl.multiple_of(token * BASES, BASES)
            value = add_token(token, cur[pl.ds(at, BASES), :], token + near_tokens)
            cur[pl.ds(at, BASES), :] = value
            n1[pl.ds(at + near, BASES), :] = normalize(value)
        return carry

    lax.fori_loop(0, tokens // 4, own_rows, 0)
    proj_copies = [
        remote(
            proj.at[pl.ds(tokens, near_tokens)], proj.at[pl.ds(0, near_tokens)],
            proj_send.at[0], proj_recv.at[0], right,
        ),
        remote(
            proj.at[pl.ds(near_tokens, near_tokens)],
            proj.at[pl.ds(tokens + near_tokens, near_tokens)],
            proj_send.at[1], proj_recv.at[1], left,
        ),
    ]
    both(proj_copies[1].start, proj_copies[0].start)
    lax.fori_loop(tokens // 4, tokens // 2, own_rows, 0)
    loads[2].wait()

    def pair_of(ref, at):
        return jnp.concatenate(
            [
                ref[pl.ds(pl.multiple_of(at, chunk), chunk), :],
                ref[pl.ds(pl.multiple_of(at + far, chunk), chunk), :],
            ],
            axis=0,
        )

    def chunk_of(step):
        return lax.rem(step + near // chunk, count)

    def halo_copy(index, side):
        at = pl.multiple_of(index * chunk, chunk)
        if side == 0:
            return remote(
                n2.at[pl.ds(at + 2 * far, chunk)], n2.at[pl.ds(at, chunk)],
                halo_send.at[0, index], halo_recv.at[0, index], right,
            )
        return remote(
            n2.at[pl.ds(at + far, chunk)], n2.at[pl.ds(at + 3 * far, chunk)],
            halo_send.at[1, index], halo_recv.at[1, index], left,
        )

    def send_chunk(step):
        index = chunk_of(step)
        both(halo_copy(index, 1).start, halo_copy(index, 0).start)

    def block_one(step, carry):
        at = pl.multiple_of(chunk_of(step) * chunk, chunk)
        window = jnp.concatenate(
            [pair_of(n1, at), pair_of(n1, at + near), pair_of(n1, at + 2 * near)], axis=1
        )
        mixed = jnp.dot(window, cw[0], preferred_element_type=F32)
        value = (pair_of(cur, at).astype(F32) + gelu(mixed)).astype(BF16)
        scaled = normalize(value)
        for part in range(2):
            rows = slice(part * chunk, (part + 1) * chunk)
            cur[pl.ds(at + part * far, chunk), :] = value[rows]
            n2[pl.ds(at + (part + 1) * far, chunk), :] = scaled[rows]

        @pl.when(step > 0)
        def _():
            send_chunk(step - 1)

        return carry

    middle = (far - near) // chunk - near // chunk
    lax.fori_loop(0, middle, block_one, 0)

    for side, edge in ((0, first_tile), (1, last_tile)):
        start = side * (tile + near)

        @pl.when(edge)
        def _():
            n1[pl.ds(start, near), :] = jnp.zeros((near, channels), BF16)
            n2[pl.ds(side * 3 * far, far), :] = jnp.zeros((far, channels), BF16)

        @pl.when(jnp.logical_not(edge))
        def _():
            raw_copies[side].wait_recv()
            proj_copies[side].wait_recv()

            def halo_rows(step, carry):
                at = pl.multiple_of(step * BASES, BASES)
                token = step + side * (tokens + near_tokens)
                n1[pl.ds(at + start, BASES), :] = normalize(
                    add_token(token, raw[side, pl.ds(at, BASES), :], token)
                )
                return carry

            lax.fori_loop(0, near_tokens, halo_rows, 0)

    lax.fori_loop(middle, count, block_one, 0)
    send_chunk(count - 1)

    lane = lax.broadcasted_iota(jnp.int32, (cands, chunk), 1)
    site_wide = jnp.concatenate([sites[...]] * (chunk // cands), axis=1)

    def tower_copy(index, part):
        rows = pl.ds(pl.multiple_of(index * chunk + part * far, chunk), chunk)
        return pltpu.make_async_copy(cur.at[rows], tower.at[rows], tower_sem.at[part, index])

    def block_two(step, carry):
        index = chunk_of(step)
        at = pl.multiple_of(index * chunk, chunk)
        both(halo_copy(index, 0).wait_recv, halo_copy(index, 1).wait_recv)
        low = n2[pl.ds(at, chunk), :]
        one = n2[pl.ds(at + far, chunk), :]
        two = n2[pl.ds(at + 2 * far, chunk), :]
        high = n2[pl.ds(at + 3 * far, chunk), :]
        window = jnp.concatenate(
            [
                jnp.concatenate([low, one], axis=0),
                jnp.concatenate([one, two], axis=0),
                jnp.concatenate([two, high], axis=0),
            ],
            axis=1,
        )
        mixed = jnp.dot(window, cw[1], preferred_element_type=F32)
        value = (pair_of(cur, at).astype(F32) + gelu(mixed)).astype(BF16)
        for part in range(2):
            cur[pl.ds(at + part * far, chunk), :] = value[part * chunk:(part + 1) * chunk]
        hits = jnp.concatenate(
            [
                jnp.where(site_wide == lane + (at + part * far), 1.0, 0.0).astype(BF16)
                for part in range(2)
            ],
            axis=1,
        )
        picked[...] += jnp.dot(hits, value, preferred_element_type=F32)
        for part in range(2):
            tower_copy(index, part).start()
        return carry

    lax.fori_loop(0, count, block_two, 0)
    loads[3].wait()
    chosen[tp] = normalize(picked[...])

    def chosen_copy(step):
        return remote(
            chosen.at[tp], chosen.at[tp], chosen_send.at[step - 1], chosen_recv.at[step - 1],
            {"ctx": ctx, "tp": peer(step)},
        )

    for step in range(1, n_tp):
        chosen_copy(step).start()

    def logit_copy(to):
        step = lax.rem(to + n_tp - tp, n_tp)
        return remote(
            logit_out.at[pl.ds(pl.multiple_of(to * 8, 8), 8)],
            logit_in.at[pl.ds(pl.multiple_of(tp * 8, 8), 8)],
            logit_send.at[step - 1], logit_recv.at[step - 1], {"ctx": ctx, "tp": to},
        )

    row = lax.broadcasted_iota(jnp.int32, wl.shape, 0)

    def heads(step, carry):
        pair = lax.rem(tp // 2 + step, n_tp // 2)
        for part in range(2):
            source = pair * 2 + part

            @pl.when(source != tp)
            def _():
                away = lax.rem(tp + n_tp - source, n_tp)
                remote(
                    chosen.at[source], chosen.at[source],
                    chosen_send.at[away - 1], chosen_recv.at[away - 1], {"ctx": ctx, "tp": source},
                ).wait_recv()

        rows_in = jnp.concatenate([chosen[pair * 2], chosen[pair * 2 + 1]], axis=0)
        scores = jnp.zeros((8, 2 * cands), F32)
        for slot in range(slots):
            hidden = gelu(jnp.dot(rows_in, hw[slot], preferred_element_type=F32)).astype(BF16)
            weights = jnp.where(row == slot, wl[...], 0.0).astype(BF16)
            scores += lax.dot_general(
                weights, hidden, (((1,), (1,)), ((), ())), preferred_element_type=F32
            )
        for part in range(2):
            source = pair * 2 + part
            logit_out[pl.ds(pl.multiple_of(source * 8, 8), 8), :] = (
                scores[:, part * cands:(part + 1) * cands]
            )
        for part in range(2):
            source = pair * 2 + part

            @pl.when(source != tp)
            def _():
                logit_copy(source).start()

        return carry

    lax.fori_loop(0, n_tp // 2, heads, 0)
    own = pl.ds(pl.multiple_of(tp * 8, 8), 8)
    logit_in[own, :] = logit_out[own, :]
    for step in range(1, n_tp):
        chosen_copy(step).wait_send()
        trunk_copies[step - 1].wait_send()
    for copies in (raw_copies, proj_copies):
        both(copies[1].wait_send, copies[0].wait_send)

    def drain(index, carry):
        both(halo_copy(index, 1).wait_send, halo_copy(index, 0).wait_send)
        return carry

    lax.fori_loop(0, count, drain, 0)

    def drain_tower(index, carry):
        for part in range(2):
            tower_copy(index, part).wait()
        return carry

    lax.fori_loop(0, count, drain_tower, 0)
    for step in range(1, n_tp):
        copy = logit_copy(peer(step))
        copy.wait_send()
        copy.wait_recv()
    for tissue_at in range(usage.shape[0]):
        slot = tissue[tissue_at]
        at = (slot // slots) * 8 + lax.rem(slot, slots)
        usage[pl.ds(tissue_at, 1), :] = logit_in[pl.ds(at, 1), :]


def on_device(
    n_ctx, n_tp,
    trunk_out, proj_weight, base_skip, conv_weight, head_hidden, head_logit, site_index, tissue_slot,
):
    tile, channels = base_skip.shape
    width = proj_weight.shape[0]
    near, far, chunk = tile // 8, tile // 2, 256
    count = far // chunk
    tokens = tile // BASES
    near_tokens = near // BASES
    cands = site_index.shape[0]
    slots, _, hidden = head_hidden.shape
    tissues = tissue_slot.shape[0]
    share = width // n_tp
    dims = (n_ctx, n_tp, tile, channels, near, far, chunk)
    anywhere = pl.BlockSpec(memory_space=pl.ANY)
    vmem = pl.BlockSpec(memory_space=pltpu.VMEM)
    smem = pl.BlockSpec(memory_space=pltpu.SMEM)
    dma = pltpu.SemaphoreType.DMA
    usage, tower = pl.pallas_call(
        functools.partial(kernel, dims),
        out_shape=(
            jax.ShapeDtypeStruct((tissues, cands), F32),
            jax.ShapeDtypeStruct((tile, channels), BF16),
        ),
        in_specs=[anywhere] * 5 + [vmem, vmem, smem],
        out_specs=(vmem, anywhere),
        scratch_shapes=[
            pltpu.VMEM((tile, channels), BF16),
            pltpu.VMEM((tile + 2 * near, channels), BF16),
            pltpu.VMEM((tile + 2 * far, channels), BF16),
            pltpu.VMEM((2, near, channels), BF16),
            pltpu.VMEM((n_tp, tokens, share), BF16),
            pltpu.VMEM((tokens + 2 * near_tokens, channels), F32),
            pltpu.VMEM((n_tp, share, channels), BF16),
            pltpu.VMEM((2, 3 * channels, channels), BF16),
            pltpu.VMEM((slots, channels, hidden), BF16),
            pltpu.VMEM((8, hidden), F32),
            pltpu.VMEM((cands, cands), jnp.int32),
            pltpu.VMEM((cands, channels), F32),
            pltpu.VMEM((n_tp, cands, channels), BF16),
            pltpu.VMEM((n_tp * 8, cands), F32),
            pltpu.VMEM((n_tp * 8, cands), F32),
            dma((5,)), dma((n_tp - 1,)), dma((n_tp - 1,)), dma((2,)), dma((2,)), dma((2,)), dma((2,)),
            dma((2, count)), dma((2, count)), dma((2, count)),
            dma((n_tp - 1,)), dma((n_tp - 1,)), dma((n_tp - 1,)), dma((n_tp - 1,)),
        ],
        compiler_params=pltpu.CompilerParams(
            collective_id=0, has_side_effects=True, vmem_limit_bytes=60 * 1024 * 1024
        ),
    )(
        trunk_out,
        proj_weight.reshape(n_tp, share, channels),
        base_skip,
        conv_weight.reshape(2, 3 * channels, channels),
        head_hidden,
        head_logit,
        site_index.reshape(1, cands),
        tissue_slot,
    )
    return usage, tower


def solution(mesh):
    return jax.shard_map(
        functools.partial(on_device, mesh.shape["ctx"], mesh.shape["tp"]),
        mesh=mesh,
        in_specs=(
            P("ctx", "tp"),
            P(),
            P(("ctx", "tp"), None),
            P(),
            P("tp", None, None),
            P("tp", None),
            P(("ctx", "tp")),
            P(),
        ),
        out_specs=(P(None, ("ctx", "tp")), P(("ctx", "tp"), None)),
        check_vma=False,
    )
```
